256 devices in a mesh: wave: 64 (over z, x, core), lev: 4 (over y).
Axes of the slice: x: 4, y: 4, z: 8, core: 2. Of those that a mesh axis runs over, the one named last changes fastest.
Arguments:
- spectral: bfloat16 [640, 2, 64, 1281], P('wave', None, 'lev'), may hold values from -6 to 6
- legendre: bfloat16 [640, 1536, 1281], P('wave', 'lev'), may hold values from -0.15625 to 0.15625
- pair_waves: int32 [640], replicated, may hold values from 0 to 639, each once
- lat_rows: int32 [1536], P('wave'), may hold values from 1 to 1280, as said below
Outputs:
- fourier: bfloat16 [1536, 2, 64, 2, 1280], P('wave', None, 'lev')
The draws below stay inside these ranges and needn't reach their ends.
Inputs may be any that keep to these rules, and one draw needn't show every extreme that they name: Slot s holds the wavenumbers pair_waves[s] and 1279 - pair_waves[s]; each value appears once. `lat_rows`: row r of the octahedral grid has 4 r + 16 points; some row is the equator row 1280.
All inputs are finite; a program needn't handle non-finite values.
Results may differ from the reference program's by a relative error of at most 0.001.
Values may be sent and summed in bfloat16 or wider, within the bound.
No kernel may reach another device: no remote copies, remote signals or barrier semaphores. Data moves between devices by JAX's collectives and lax.ppermute only.
A program may use at most 192 MiB of HBM per device.

```python
import jax
import jax.numpy as jnp
from jax import lax

TRUNC = 1279
FIELDS = 64
WAVES = 1280
PAIRS = 640
DEGREES = 1281
ROWS = 1536


def draw_lat_rows(key, part):
    row_numbers = jax.random.randint(jax.random.fold_in(key, 1), (ROWS,), 1, WAVES + 1)
    equator_at = jax.random.randint(jax.random.fold_in(key, 2), (), 0, ROWS)
    return row_numbers.at[equator_at].set(WAVES).astype(jnp.int32)


def block_scale(rng, dims, shards, least, top_value):
    level = 1.0
    for position, parts in shards:
        steps = jax.random.uniform(jax.random.fold_in(jax.random.fold_in(rng, 6), position), (parts,), jnp.float32, least / len(shards), top_value / len(shards))
        level = level * jnp.repeat(jnp.exp(steps), dims[position] // parts).reshape((-1,) + (1,) * (len(dims) - 1 - position))
    return level


def scatter_about(key, shape, spread, reach, pieces=(), kind=jnp.bfloat16):
    level = block_scale(key, shape, pieces, -0.22, 0.18) if pieces else 1.0
    result = jax.random.normal(key, shape, jnp.float32) * spread * level
    return jnp.minimum(jnp.maximum(result, -reach), reach).astype(kind)


def setup_inputs(seed: int = 0) -> dict:
    keys = jax.random.split(jax.random.key(seed), 5)
    spectral = scatter_about(keys[0], (PAIRS, 2, FIELDS, DEGREES), 1.0, 6.0, ((0, 64), (2, 4)))
    legendre = scatter_about(keys[1], (PAIRS, ROWS, DEGREES), WAVES ** -0.5, 0.15625, ((0, 64), (1, 4)))
    pair_waves = jax.random.permutation(keys[2], PAIRS).astype(jnp.int32)
    lat_rows = draw_lat_rows(jax.random.fold_in(keys[4], 71), 0)
    return dict(spectral=spectral, legendre=legendre, pair_waves=pair_waves, lat_rows=lat_rows)


def one_pair(inputs):
    coeffs, weights, low_wave = inputs
    degree_index = jnp.arange(DEGREES, dtype=jnp.int32)
    split_at = WAVES - low_wave
    in_first = degree_index < split_at
    members = jnp.stack([in_first, jnp.logical_not(in_first)]).astype(jnp.float32)
    coeff_wide = coeffs.astype(jnp.float32)
    weight_wide = weights.astype(jnp.float32)
    masked = members[:, None, None, :] * coeff_wide[None]
    even_sum = jnp.einsum("abfk,rk->abfr", masked[..., 0::2], weight_wide[:, 0::2], precision=lax.Precision.HIGHEST)
    odd_sum = jnp.einsum("abfk,rk->abfr", masked[..., 1::2], weight_wide[:, 1::2], precision=lax.Precision.HIGHEST)
    south_sign = jnp.where(split_at % 2 == 0, jnp.float32(1.0), jnp.float32(-1.0))
    member_sign = jnp.stack([jnp.ones_like(south_sign), south_sign])
    northern = even_sum + odd_sum
    southern = (even_sum - odd_sum) * member_sign[:, None, None, None]
    return jnp.stack([northern, southern], axis=1).astype(jnp.bfloat16)


def reference(spectral, legendre, pair_waves, lat_rows):
    fourier_pairs = lax.map(one_pair, (spectral, legendre, pair_waves))
    inverse = jnp.zeros((PAIRS,), jnp.int32).at[pair_waves].set(jnp.arange(PAIRS, dtype=jnp.int32))
    wavenumbers = jnp.arange(WAVES, dtype=jnp.int32)
    low_pick = inverse[jnp.clip(wavenumbers, 0, PAIRS - 1)]
    high_pick = PAIRS + inverse[jnp.clip(WAVES - 1 - wavenumbers, 0, PAIRS - 1)]
    wave_index = jnp.where(wavenumbers < PAIRS, low_pick, high_pick).astype(jnp.int32)
    flattened = jnp.transpose(fourier_pairs, (5, 2, 4, 3, 1, 0)).reshape(ROWS, 2, FIELDS, 2, 2 * PAIRS)
    placed = jnp.take(flattened, wave_index, axis=4)
    cutoff = jnp.minimum(TRUNC, 2 * lat_rows + 7)
    kept_mask = wavenumbers[None, :] <= cutoff[:, None]
    return jnp.where(kept_mask[:, None, None, None, :], placed, jnp.zeros((), jnp.bfloat16))
```

```python
import jax
import jax.numpy as jnp
from jax import lax
from jax.experimental import pallas as pl
from jax.experimental.pallas import tpu as pltpu
from jax.sharding import PartitionSpec as P

TRUNC = 1279
WAVES = 1280
HALF = 640
LANES = 128
CHUNKS = (2, 4, 4)
STEP = 2
VMEM_LIMIT = 48 * 1024 * 1024


def synthesis_kernel(low_ref, *refs):
    levs = (len(refs) - 1) // 2
    spectral_refs = refs[:levs]
    legendre_ref = refs[levs]
    out_refs = refs[levs + 1 :]
    degrees, rows = legendre_ref.shape[1:]
    blocks = out_refs[0].shape[0]
    block_rows = rows // blocks
    step = pl.program_id(0)
    degree_index = lax.broadcasted_iota(jnp.int32, (1, degrees), 1)
    sums = []
    for pair in range(STEP):
        split_at = WAVES - low_ref[step * STEP + pair]
        first = jnp.where(degree_index < split_at, 1.0, 0.0).astype(jnp.float32)
        second = 1.0 - first
        sign_first = (1 - 2 * (degree_index % 2)).astype(jnp.float32)
        sign_second = sign_first * (1 - 2 * (split_at % 2)).astype(jnp.float32)
        factors = [first, first * sign_first, second, second * sign_second]
        factors = [factor.astype(jnp.bfloat16) for factor in factors]
        masked = []
        for spectral_ref in spectral_refs:
            coeffs = spectral_ref[pair]
            masked += [coeffs * factor for factor in factors]
        masked = jnp.concatenate(masked, axis=0)
        sums.append(jnp.dot(masked, legendre_ref[pair], preferred_element_type=jnp.float32))
    for lev in range(levs):
        turned = [total[lev * LANES : (lev + 1) * LANES].T for total in sums]
        for block in range(blocks):
            top = block * block_rows
            parts = [part[top : top + block_rows] for part in turned]
            out_refs[lev][block] = jnp.concatenate(parts, axis=0).astype(jnp.bfloat16)


def synthesis(low_waves, spectral, legendre, first_pair, block_rows):
    pairs, columns, degrees = spectral[0].shape
    rows = legendre.shape[2]
    blocks = rows // block_rows
    first_step = first_pair // STEP
    coeff_spec = pl.BlockSpec((STEP, columns, degrees), lambda i, low: (i, 0, 0))
    out_spec = pl.BlockSpec((blocks, STEP * block_rows, LANES), lambda i, low: (0, i, 0))
    out_shape = jax.ShapeDtypeStruct((blocks, pairs * block_rows, LANES), jnp.bfloat16)
    return pl.pallas_call(
        synthesis_kernel,
        grid_spec=pltpu.PrefetchScalarGridSpec(
            num_scalar_prefetch=1,
            grid=(pairs // STEP,),
            in_specs=[coeff_spec] * len(spectral)
            + [pl.BlockSpec((STEP, degrees, rows), lambda i, low: (i + first_step, 0, 0))],
            out_specs=[out_spec] * len(spectral),
        ),
        out_shape=[out_shape] * len(spectral),
        compiler_params=pltpu.CompilerParams(vmem_limit_bytes=VMEM_LIMIT),
        name="synthesis",
    )(low_waves, *spectral, legendre)


def joining_kernel(at_ref, *refs):
    out_ref = refs[-1]
    for item, ref in enumerate(refs[:-1]):
        out_ref[at_ref[item]] = ref[...]


def joining(at, pieces):
    shape = (len(pieces),) + pieces[0].shape
    return pl.pallas_call(
        joining_kernel,
        in_specs=[pl.BlockSpec(memory_space=pltpu.SMEM)]
        + [pl.BlockSpec(memory_space=pltpu.VMEM)] * len(pieces),
        out_specs=pl.BlockSpec(memory_space=pltpu.VMEM),
        out_shape=jax.ShapeDtypeStruct(shape, jnp.bfloat16),
        compiler_params=pltpu.CompilerParams(vmem_limit_bytes=VMEM_LIMIT),
        name="joining",
    )(at, *pieces)


def turning_kernel(wire_ref, out_ref, wide_ref, *, block_rows):
    members, group_rows, slots = out_ref.shape
    half = LANES // 2
    group = group_rows // half
    step = pl.program_id(0)

    @pl.when(step == 0)
    def _():
        wide_ref[...] = wire_ref[...].astype(jnp.float32)

    for item in range(group):
        picked = wide_ref[pl.ds(step * group + item, slots, stride=block_rows), :]
        turned = picked.T.astype(jnp.bfloat16)
        for member in range(members):
            out_ref[member, pl.ds(item * half, half), :] = turned[member * half : (member + 1) * half]


def turning(wire, block_rows):
    half = LANES // 2
    slots = wire.shape[0] // block_rows
    group = 6
    return pl.pallas_call(
        lambda *refs: turning_kernel(*refs, block_rows=block_rows),
        grid=(block_rows // group,),
        in_specs=[pl.BlockSpec(wire.shape, lambda i: (0, 0))],
        out_specs=pl.BlockSpec((2, group * half, slots), lambda i: (0, i, 0)),
        out_shape=jax.ShapeDtypeStruct((2, block_rows * half, slots), jnp.bfloat16),
        scratch_shapes=[pltpu.VMEM(wire.shape, jnp.float32)],
        compiler_params=pltpu.CompilerParams(vmem_limit_bytes=VMEM_LIMIT),
        name="turning",
    )(wire)


def placing_kernel(cutoff_ref, *refs):
    count = (len(refs) - 1) // 4
    slot_refs = refs[:count]
    turned_refs = refs[count : 2 * count]
    out_ref = refs[2 * count]
    place_refs = refs[2 * count + 1 :]
    step = pl.program_id(0)
    half = LANES // 2
    group = turned_refs[0].shape[1] // half

    @pl.when(step == 0)
    def _():
        for item in range(count):
            slots = slot_refs[item][...]
            waves = lax.broadcasted_iota(jnp.int32, (slots.shape[0], HALF), 1)
            place_refs[2 * item][...] = jnp.where(slots == waves, 1.0, 0.0).astype(jnp.bfloat16)
            place_refs[2 * item + 1][...] = jnp.where(
                slots == HALF - 1 - waves, 1.0, 0.0
            ).astype(jnp.bfloat16)

    for member in range(2):
        placed = None
        for item in range(count):
            part = jnp.dot(
                turned_refs[item][member],
                place_refs[2 * item + member][...],
                preferred_element_type=jnp.float32,
            )
            placed = part if placed is None else placed + part
        waves = lax.broadcasted_iota(jnp.int32, (half, HALF), 1) + member * HALF
        for row in range(group):
            kept = waves <= cutoff_ref[step * group + row]
            part = jnp.where(kept, placed[row * half : (row + 1) * half], 0.0).astype(jnp.bfloat16)
            out_ref[pl.ds(row * half // 2, half // 2), :, pl.ds(member * HALF, HALF)] = part.reshape(
                half // 2, 2, HALF
            )


def placing(cutoff, slots, turned):
    block_rows = cutoff.shape[0]
    group = 4
    half = LANES // 2
    return pl.pallas_call(
        placing_kernel,
        grid_spec=pltpu.PrefetchScalarGridSpec(
            num_scalar_prefetch=1,
            grid=(block_rows // group,),
            in_specs=[pl.BlockSpec(s.shape, lambda i, cut: (0, 0)) for s in slots]
            + [pl.BlockSpec((2, group * half, t.shape[2]), lambda i, cut: (0, i, 0)) for t in turned],
            out_specs=pl.BlockSpec((group * half // 2, 2, WAVES), lambda i, cut: (i, 0, 0)),
            scratch_shapes=[
                pltpu.VMEM((s.shape[0], HALF), jnp.bfloat16) for s in slots for _ in range(2)
            ],
        ),
        out_shape=jax.ShapeDtypeStruct((block_rows * half // 2, 2, WAVES), jnp.bfloat16),
        compiler_params=pltpu.CompilerParams(vmem_limit_bytes=VMEM_LIMIT),
        name="placing",
    )(cutoff, *slots, *turned)


def body(spectral, legendre, pair_waves, lat_rows):
    pairs_dev, parts, fields, degrees = spectral.shape
    block_rows = lat_rows.shape[0]
    levs = lax.axis_size("lev")
    waves = lax.axis_size("wave")
    lev = lax.axis_index("lev")
    first_slot = lax.axis_index("wave") * pairs_dev
    cutoff = jnp.minimum(TRUNC, 2 * lat_rows + 7)
    legendre = legendre.transpose(0, 2, 1)
    source = (lev - jnp.arange(levs, dtype=jnp.int32)) % levs
    slot_table = pair_waves.reshape(waves, pairs_dev)

    def shifted(x, by):
        return lax.ppermute(x, "lev", [(k, (k + by) % levs) for k in range(levs)])

    def ordered(first, last):
        own = spectral[first:last].transpose(0, 2, 1, 3)
        return own.reshape(last - first, fields * parts, degrees)

    later = lax.all_gather(ordered(CHUNKS[0], pairs_dev), "lev", axis=0, tiled=False)
    slots, turned = [], []
    first = 0
    for pairs in CHUNKS:
        if first == 0:
            own = ordered(0, pairs)
            coeffs = [own] + [shifted(own, -by) for by in range(1, levs)]
        else:
            at = [(lev + by) % levs for by in range(levs)]
            coeffs = [
                lax.dynamic_slice(later, (a, first - CHUNKS[0], 0, 0), (1, pairs) + later.shape[2:])[0]
                for a in at
            ]
        low_waves = lax.dynamic_slice_in_dim(pair_waves, first_slot + first, pairs)
        pieces = synthesis(low_waves, coeffs, legendre, first, block_rows)
        pieces = [pieces[0]] + [shifted(pieces[by], by) for by in range(1, levs)]
        wire = joining(source, pieces)
        wire = wire.reshape((-1,) + wire.shape[2:])
        wire = lax.all_to_all(wire, "wave", 0, 0, tiled=True)
        turned.append(turning(wire.reshape(-1, LANES), block_rows))
        slots.append(slot_table[:, first : first + pairs].reshape(-1, 1))
        first += pairs
    placed = placing(cutoff, slots, turned)
    return placed.reshape(block_rows, 2, fields, parts, WAVES)


def solution(mesh):
    return jax.shard_map(
        body,
        mesh=mesh,
        in_specs=(P("wave", None, "lev", None), P("wave", "lev", None), P(), P("wave")),
        out_specs=P("wave", None, "lev", None, None),
        check_vma=False,
    )
```

```python
import jax
import jax.numpy as jnp
from jax import lax
from jax.experimental import pallas as pl
from jax.experimental.pallas import tpu as pltpu
from jax.sharding import PartitionSpec as P

TRUNC = 1279
WAVES = 1280
HALF = 640
LANES = 128
CHUNKS = (4,6)
STEP = 2
VMEM_LIMIT = 48 * 1024 * 1024


def synthesis_kernel(low_ref, *refs):
    levs = (len(refs) - 1) // 2
    spectral_refs = refs[:levs]
    legendre_ref = refs[levs]
    out_refs = refs[levs + 1 :]
    degrees, rows = legendre_ref.shape[1:]
    blocks = out_refs[0].shape[0]
    block_rows = rows // blocks
    step = pl.program_id(0)
    degree_index = lax.broadcasted_iota(jnp.int32, (1, degrees), 1)
    sums = []
    for pair in range(STEP):
        split_at = WAVES - low_ref[step * STEP + pair]
        first = jnp.where(degree_index < split_at, 1.0, 0.0).astype(jnp.float32)
        second = 1.0 - first
        sign_first = (1 - 2 * (degree_index % 2)).astype(jnp.float32)
        sign_second = sign_first * (1 - 2 * (split_at % 2)).astype(jnp.float32)
        factors = [first, first * sign_first, second, second * sign_second]
        factors = [factor.astype(jnp.bfloat16) for factor in factors]
        masked = []
        for spectral_ref in spectral_refs:
            coeffs = spectral_ref[pair]
            masked += [coeffs * factor for factor in factors]
        masked = jnp.concatenate(masked, axis=0)
        sums.append(jnp.dot(masked, legendre_ref[pair], preferred_element_type=jnp.float32))
    for lev in range(levs):
        turned = [total[lev * LANES : (lev + 1) * LANES].T for total in sums]
        for block in range(blocks):
            top = block * block_rows
            parts = [part[top : top + block_rows] for part in turned]
            out_refs[lev][block] = jnp.concatenate(parts, axis=0).astype(jnp.bfloat16)


def synthesis(low_waves, spectral, legendre, first_pair, block_rows):
    pairs, columns, degrees = spectral[0].shape
    rows = legendre.shape[2]
    blocks = rows // block_rows
    first_step = first_pair // STEP
    coeff_spec = pl.BlockSpec((STEP, columns, degrees), lambda i, low: (i, 0, 0))
    out_spec = pl.BlockSpec((blocks, STEP * block_rows, LANES), lambda i, low: (0, i, 0))
    out_shape = jax.ShapeDtypeStruct((blocks, pairs * block_rows, LANES), jnp.bfloat16)
    return pl.pallas_call(
        synthesis_kernel,
        grid_spec=pltpu.PrefetchScalarGridSpec(
            num_scalar_prefetch=1,
            grid=(pairs // STEP,),
            in_specs=[coeff_spec] * len(spectral)
            + [pl.BlockSpec((STEP, degrees, rows), lambda i, low: (i + first_step, 0, 0))],
            out_specs=[out_spec] * len(spectral),
        ),
        out_shape=[out_shape] * len(spectral),
        compiler_params=pltpu.CompilerParams(vmem_limit_bytes=VMEM_LIMIT),
        name="synthesis",
    )(low_waves, *spectral, legendre)


def joining_kernel(at_ref, *refs):
    out_ref = refs[-1]
    for item, ref in enumerate(refs[:-1]):
        out_ref[at_ref[item]] = ref[...]


def joining(at, pieces):
    shape = (len(pieces),) + pieces[0].shape
    return pl.pallas_call(
        joining_kernel,
        in_specs=[pl.BlockSpec(memory_space=pltpu.SMEM)]
        + [pl.BlockSpec(memory_space=pltpu.VMEM)] * len(pieces),
        out_specs=pl.BlockSpec(memory_space=pltpu.VMEM),
        out_shape=jax.ShapeDtypeStruct(shape, jnp.bfloat16),
        compiler_params=pltpu.CompilerParams(vmem_limit_bytes=VMEM_LIMIT),
        name="joining",
    )(at, *pieces)


def turning_kernel(wire_ref, out_ref, wide_ref, *, block_rows):
    members, group_rows, slots = out_ref.shape
    half = LANES // 2
    group = group_rows // half
    step = pl.program_id(0)

    @pl.when(step == 0)
    def _():
        wide_ref[...] = wire_ref[...].astype(jnp.float32)

    for item in range(group):
        picked = wide_ref[pl.ds(step * group + item, slots, stride=block_rows), :]
        turned = picked.T.astype(jnp.bfloat16)
        for member in range(members):
            out_ref[member, pl.ds(item * half, half), :] = turned[member * half : (member + 1) * half]


def turning(wire, block_rows):
    half = LANES // 2
    slots = wire.shape[0] // block_rows
    group = 6
    return pl.pallas_call(
        lambda *refs: turning_kernel(*refs, block_rows=block_rows),
        grid=(block_rows // group,),
        in_specs=[pl.BlockSpec(wire.shape, lambda i: (0, 0))],
        out_specs=pl.BlockSpec((2, group * half, slots), lambda i: (0, i, 0)),
        out_shape=jax.ShapeDtypeStruct((2, block_rows * half, slots), jnp.bfloat16),
        scratch_shapes=[pltpu.VMEM(wire.shape, jnp.float32)],
        compiler_params=pltpu.CompilerParams(vmem_limit_bytes=VMEM_LIMIT),
        name="turning",
    )(wire)


def placing_kernel(cutoff_ref, *refs):
    count = (len(refs) - 1) // 4
    slot_refs = refs[:count]
    turned_refs = refs[count : 2 * count]
    out_ref = refs[2 * count]
    place_refs = refs[2 * count + 1 :]
    step = pl.program_id(0)
    half = LANES // 2
    group = turned_refs[0].shape[1] // half

    @pl.when(step == 0)
    def _():
        for item in range(count):
            slots = slot_refs[item][...]
            waves = lax.broadcasted_iota(jnp.int32, (slots.shape[0], HALF), 1)
            place_refs[2 * item][...] = jnp.where(slots == waves, 1.0, 0.0).astype(jnp.bfloat16)
            place_refs[2 * item + 1][...] = jnp.where(
                slots == HALF - 1 - waves, 1.0, 0.0
            ).astype(jnp.bfloat16)

    for member in range(2):
        placed = None
        for item in range(count):
            part = jnp.dot(
                turned_refs[item][member],
                place_refs[2 * item + member][...],
                preferred_element_type=jnp.float32,
            )
            placed = part if placed is None else placed + part
        waves = lax.broadcasted_iota(jnp.int32, (half, HALF), 1) + member * HALF
        for row in range(group):
            kept = waves <= cutoff_ref[step * group + row]
            part = jnp.where(kept, placed[row * half : (row + 1) * half], 0.0).astype(jnp.bfloat16)
            out_ref[pl.ds(row * half // 2, half // 2), :, pl.ds(member * HALF, HALF)] = part.reshape(
                half // 2, 2, HALF
            )


def placing(cutoff, slots, turned):
    block_rows = cutoff.shape[0]
    group = 4
    half = LANES // 2
    return pl.pallas_call(
        placing_kernel,
        grid_spec=pltpu.PrefetchScalarGridSpec(
            num_scalar_prefetch=1,
            grid=(block_rows // group,),
            in_specs=[pl.BlockSpec(s.shape, lambda i, cut: (0, 0)) for s in slots]
            + [pl.BlockSpec((2, group * half, t.shape[2]), lambda i, cut: (0, i, 0)) for t in turned],
            out_specs=pl.BlockSpec((group * half // 2, 2, WAVES), lambda i, cut: (i, 0, 0)),
            scratch_shapes=[
                pltpu.VMEM((s.shape[0], HALF), jnp.bfloat16) for s in slots for _ in range(2)
            ],
        ),
        out_shape=jax.ShapeDtypeStruct((block_rows * half // 2, 2, WAVES), jnp.bfloat16),
        compiler_params=pltpu.CompilerParams(vmem_limit_bytes=VMEM_LIMIT),
        name="placing",
    )(cutoff, *slots, *turned)


def body(spectral, legendre, pair_waves, lat_rows):
    pairs_dev, parts, fields, degrees = spectral.shape
    block_rows = lat_rows.shape[0]
    levs = lax.axis_size("lev")
    waves = lax.axis_size("wave")
    lev = lax.axis_index("lev")
    first_slot = lax.axis_index("wave") * pairs_dev
    cutoff = jnp.minimum(TRUNC, 2 * lat_rows + 7)
    legendre = legendre.transpose(0, 2, 1)
    source = (lev - jnp.arange(levs, dtype=jnp.int32)) % levs
    slot_table = pair_waves.reshape(waves, pairs_dev)

    def shifted(x, by):
        return lax.ppermute(x, "lev", [(k, (k + by) % levs) for k in range(levs)])

    coeffs, firsts, slots = [], [], []
    first = 0
    for pairs in CHUNKS:
        own = spectral[first : first + pairs].transpose(0, 2, 1, 3)
        own = own.reshape(pairs, fields * parts, degrees)
        above, below = shifted(own, -1), shifted(own, 1)
        cut = pairs // 2
        across = jnp.concatenate([shifted(above[:cut], -1), shifted(below[cut:], 1)], axis=0)
        coeffs.append([own, above, across, below])
        firsts.append(first)
        slots.append(slot_table[:, first : first + pairs].reshape(-1, 1))
        first += pairs

    turned = []
    for item, pairs in enumerate(CHUNKS):
        first = firsts[item]
        low_waves = lax.dynamic_slice_in_dim(pair_waves, first_slot + first, pairs)
        pieces = synthesis(low_waves, coeffs[item], legendre, first, block_rows)
        pieces = [pieces[0]] + [shifted(pieces[by], by) for by in range(1, levs)]
        if item + 1 < len(CHUNKS):
            pieces, coeffs[item + 1] = lax.optimization_barrier((pieces, coeffs[item + 1]))
        wire = joining(source, pieces)
        wire = wire.reshape((-1,) + wire.shape[2:])
        wire = lax.all_to_all(wire, "wave", 0, 0, tiled=True)
        turned.append(turning(wire.reshape(-1, LANES), block_rows))
    placed = placing(cutoff, slots, turned)
    return placed.reshape(block_rows, 2, fields, parts, WAVES)


def solution(mesh):
    return jax.shard_map(
        body,
        mesh=mesh,
        in_specs=(P("wave", None, "lev", None), P("wave", "lev", None), P(), P("wave")),
        out_specs=P("wave", None, "lev", None, None),
        check_vma=False,
    )
```

```python
import jax
import jax.numpy as jnp
from jax import lax
from jax.experimental import pallas as pl
from jax.experimental.pallas import tpu as pltpu
from jax.sharding import PartitionSpec as P

TRUNC = 1279
WAVES = 1280
HALF = 640
LANES = 128
CHUNKS = (3,7)
STEP = 1
VMEM_LIMIT = 48 * 1024 * 1024


def synthesis_kernel(low_ref, *refs):
    levs = (len(refs) - 1) // 2
    spectral_refs = refs[:levs]
    legendre_ref = refs[levs]
    out_refs = refs[levs + 1 :]
    degrees, rows = legendre_ref.shape[1:]
    blocks = out_refs[0].shape[0]
    block_rows = rows // blocks
    step = pl.program_id(0)
    degree_index = lax.broadcasted_iota(jnp.int32, (1, degrees), 1)
    sums = []
    for pair in range(STEP):
        split_at = WAVES - low_ref[step * STEP + pair]
        first = jnp.where(degree_index < split_at, 1.0, 0.0).astype(jnp.float32)
        second = 1.0 - first
        sign_first = (1 - 2 * (degree_index % 2)).astype(jnp.float32)
        sign_second = sign_first * (1 - 2 * (split_at % 2)).astype(jnp.float32)
        factors = [first, first * sign_first, second, second * sign_second]
        factors = [factor.astype(jnp.bfloat16) for factor in factors]
        masked = []
        for spectral_ref in spectral_refs:
            coeffs = spectral_ref[pair]
            masked += [coeffs * factor for factor in factors]
        masked = jnp.concatenate(masked, axis=0)
        sums.append(jnp.dot(masked, legendre_ref[pair], preferred_element_type=jnp.float32))
    for lev in range(levs):
        turned = [total[lev * LANES : (lev + 1) * LANES].T for total in sums]
        for block in range(blocks):
            top = block * block_rows
            parts = [part[top : top + block_rows] for part in turned]
            out_refs[lev][block] = jnp.concatenate(parts, axis=0).astype(jnp.bfloat16)


def synthesis(low_waves, spectral, legendre, first_pair, skipped, block_rows):
    pairs = low_waves.shape[0]
    columns, degrees = spectral[0].shape[1:]
    skipped_steps = skipped // STEP
    rows = legendre.shape[2]
    blocks = rows // block_rows
    first_step = first_pair // STEP
    coeff_spec = pl.BlockSpec((STEP, columns, degrees), lambda i, low: (i + skipped_steps, 0, 0))
    out_spec = pl.BlockSpec((blocks, STEP * block_rows, LANES), lambda i, low: (0, i, 0))
    out_shape = jax.ShapeDtypeStruct((blocks, pairs * block_rows, LANES), jnp.bfloat16)
    return pl.pallas_call(
        synthesis_kernel,
        grid_spec=pltpu.PrefetchScalarGridSpec(
            num_scalar_prefetch=1,
            grid=(pairs // STEP,),
            in_specs=[coeff_spec] * len(spectral)
            + [pl.BlockSpec((STEP, degrees, rows), lambda i, low: (i + first_step, 0, 0))],
            out_specs=[out_spec] * len(spectral),
        ),
        out_shape=[out_shape] * len(spectral),
        compiler_params=pltpu.CompilerParams(vmem_limit_bytes=VMEM_LIMIT),
        name="synthesis",
    )(low_waves, *spectral, legendre)


def joining_kernel(at_ref, *refs):
    out_ref = refs[-1]
    for item, ref in enumerate(refs[:-1]):
        out_ref[at_ref[item]] = ref[...]


def joining(at, pieces):
    shape = (len(pieces),) + pieces[0].shape
    return pl.pallas_call(
        joining_kernel,
        in_specs=[pl.BlockSpec(memory_space=pltpu.SMEM)]
        + [pl.BlockSpec(memory_space=pltpu.VMEM)] * len(pieces),
        out_specs=pl.BlockSpec(memory_space=pltpu.VMEM),
        out_shape=jax.ShapeDtypeStruct(shape, jnp.bfloat16),
        compiler_params=pltpu.CompilerParams(vmem_limit_bytes=VMEM_LIMIT),
        name="joining",
    )(at, *pieces)


def turning_kernel(wire_ref, out_ref, wide_ref, *, block_rows):
    members, group_rows, slots = out_ref.shape
    half = LANES // 2
    group = group_rows // half
    step = pl.program_id(0)

    @pl.when(step == 0)
    def _():
        wide_ref[...] = wire_ref[...].astype(jnp.float32)

    for item in range(group):
        picked = wide_ref[pl.ds(step * group + item, slots, stride=block_rows), :]
        turned = picked.T.astype(jnp.bfloat16)
        for member in range(members):
            out_ref[member, pl.ds(item * half, half), :] = turned[member * half : (member + 1) * half]


def turning(wire, block_rows):
    half = LANES // 2
    slots = wire.shape[0] // block_rows
    group = 6
    return pl.pallas_call(
        lambda *refs: turning_kernel(*refs, block_rows=block_rows),
        grid=(block_rows // group,),
        in_specs=[pl.BlockSpec(wire.shape, lambda i: (0, 0))],
        out_specs=pl.BlockSpec((2, group * half, slots), lambda i: (0, i, 0)),
        out_shape=jax.ShapeDtypeStruct((2, block_rows * half, slots), jnp.bfloat16),
        scratch_shapes=[pltpu.VMEM(wire.shape, jnp.float32)],
        compiler_params=pltpu.CompilerParams(vmem_limit_bytes=VMEM_LIMIT),
        name="turning",
    )(wire)


def placing_kernel(cutoff_ref, *refs):
    count = (len(refs) - 1) // 4
    slot_refs = refs[:count]
    turned_refs = refs[count : 2 * count]
    out_ref = refs[2 * count]
    place_refs = refs[2 * count + 1 :]
    step = pl.program_id(0)
    half = LANES // 2
    group = turned_refs[0].shape[1] // half

    @pl.when(step == 0)
    def _():
        for item in range(count):
            slots = slot_refs[item][...]
            waves = lax.broadcasted_iota(jnp.int32, (slots.shape[0], HALF), 1)
            place_refs[2 * item][...] = jnp.where(slots == waves, 1.0, 0.0).astype(jnp.bfloat16)
            place_refs[2 * item + 1][...] = jnp.where(
                slots == HALF - 1 - waves, 1.0, 0.0
            ).astype(jnp.bfloat16)

    for member in range(2):
        placed = None
        for item in range(count):
            part = jnp.dot(
                turned_refs[item][member],
                place_refs[2 * item + member][...],
                preferred_element_type=jnp.float32,
            )
            placed = part if placed is None else placed + part
        waves = lax.broadcasted_iota(jnp.int32, (half, HALF), 1) + member * HALF
        for row in range(group):
            kept = waves <= cutoff_ref[step * group + row]
            part = jnp.where(kept, placed[row * half : (row + 1) * half], 0.0).astype(jnp.bfloat16)
            out_ref[pl.ds(row * half // 2, half // 2), :, pl.ds(member * HALF, HALF)] = part.reshape(
                half // 2, 2, HALF
            )


def placing(cutoff, slots, turned):
    block_rows = cutoff.shape[0]
    group = 4
    half = LANES // 2
    return pl.pallas_call(
        placing_kernel,
        grid_spec=pltpu.PrefetchScalarGridSpec(
            num_scalar_prefetch=1,
            grid=(block_rows // group,),
            in_specs=[pl.BlockSpec(s.shape, lambda i, cut: (0, 0)) for s in slots]
            + [pl.BlockSpec((2, group * half, t.shape[2]), lambda i, cut: (0, i, 0)) for t in turned],
            out_specs=pl.BlockSpec((group * half // 2, 2, WAVES), lambda i, cut: (i, 0, 0)),
            scratch_shapes=[
                pltpu.VMEM((s.shape[0], HALF), jnp.bfloat16) for s in slots for _ in range(2)
            ],
        ),
        out_shape=jax.ShapeDtypeStruct((block_rows * half // 2, 2, WAVES), jnp.bfloat16),
        compiler_params=pltpu.CompilerParams(vmem_limit_bytes=VMEM_LIMIT),
        name="placing",
    )(cutoff, *slots, *turned)


def body(spectral, legendre, pair_waves, lat_rows):
    pairs_dev, parts, fields, degrees = spectral.shape
    block_rows = lat_rows.shape[0]
    levs = lax.axis_size("lev")
    waves = lax.axis_size("wave")
    lev = lax.axis_index("lev")
    first_slot = lax.axis_index("wave") * pairs_dev
    cutoff = jnp.minimum(TRUNC, 2 * lat_rows + 7)
    legendre = legendre.transpose(0, 2, 1)
    source = (lev - jnp.arange(levs, dtype=jnp.int32)) % levs
    slot_table = pair_waves.reshape(waves, pairs_dev)

    def shifted(x, by):
        return lax.ppermute(x, "lev", [(k, (k + by) % levs) for k in range(levs)])

    def spread(first, last):
        own = spectral[first:last].transpose(0, 2, 1, 3)
        own = own.reshape(last - first, fields * parts, degrees)
        above, below = shifted(own, -1), shifted(own, 1)
        cut = (last - first) // 2
        across = [shifted(above[:cut], -1), shifted(below[cut:], 1)]
        return [own, above, jnp.concatenate(across, axis=0), below]

    def summed(coeffs, first, skipped, pairs):
        low_waves = lax.dynamic_slice_in_dim(pair_waves, first_slot + first, pairs)
        return synthesis(low_waves, coeffs, legendre, first, skipped, block_rows)

    def exchanged(pieces):
        return [pieces[0]] + [shifted(pieces[by], by) for by in range(1, levs)]

    early = CHUNKS[0]
    coeffs = spread(0, early)
    later = spread(early, pairs_dev)
    arrived = [exchanged(summed(coeffs, 0, 0, early))]
    first = early
    for item, pairs in enumerate(CHUNKS[1:]):
        sums = summed(later, first, first - early, pairs)
        if item == 0:
            arrived[0], sums = lax.optimization_barrier((arrived[0], sums))
        arrived.append(exchanged(sums))
        first += pairs
    slots, turned = [], []
    first = 0
    for item, pairs in enumerate(CHUNKS):
        pieces = arrived[item]
        wire = joining(source, pieces)
        wire = wire.reshape((-1,) + wire.shape[2:])
        wire = lax.all_to_all(wire, "wave", 0, 0, tiled=True)
        turned.append(turning(wire.reshape(-1, LANES), block_rows))
        slots.append(slot_table[:, first : first + pairs].reshape(-1, 1))
        first += pairs
    placed = placing(cutoff, slots, turned)
    return placed.reshape(block_rows, 2, fields, parts, WAVES)


def solution(mesh):
    return jax.shard_map(
        body,
        mesh=mesh,
        in_specs=(P("wave", None, "lev", None), P("wave", "lev", None), P(), P("wave")),
        out_specs=P("wave", None, "lev", None, None),
        check_vma=False,
    )
```
